32 devices in a mesh: year: 4 (over z), row: 2 (over x), col: 4 (over y, core).
Axes of the slice: x: 2, y: 2, z: 4, core: 2. Of those that a mesh axis runs over, the one named last changes fastest.
Arguments:
- observed: float32 [4, 46, 128, 512], P('year', None, 'row', 'col'), may hold values from 0 to 0.8
- quality: int32 [4, 46, 128, 512], P('year', None, 'row', 'col'), may hold values from 0 to 3, as said below
- land_mask: int32 [128, 512], P('row', 'col'), may hold values 0 or 1
- params: float32 [4, 7, 128, 512], P('year', None, 'row', 'col'), may hold values from -0.3 to 3.4
- spatial_weight: float32 [7], replicated, may hold values from 0.2 to 2
- temporal_weight: float32 [7], replicated, may hold values from 0.2 to 2
Outputs:
- new_params: float32 [4, 7, 128, 512], P('year', None, 'row', 'col')
- residual: float32 [4, 7, 128, 512], P('year', None, 'row', 'col')
The draws below stay inside these ranges and needn't reach their ends.
Inputs may be any that keep to these rules, and one draw needn't show every extreme that they name: `quality`: 0 good, 1 marginal, 2 snow, 3 cloud.
All inputs are finite; a program needn't handle non-finite values. No bound on the sum of `land_mask` on one device may be relied on, other than what follows from the above.
Results may differ from the reference program's by a relative error of at most 0.0003.
Values sent between devices are 32-bit elements; how exact they have to be, the bound alone decides.
A program may use at most 64 MiB of HBM per device.

```python
import math
import jax
import jax.numpy as jnp
from jax import lax

DATES = 46
PARAMS = 7
ITERS = 4
YEARS = 4
NR = 128
NC = 512


def draw_quality(key, part):
    base_key = jax.random.fold_in(key, 11)
    level_key, other_key = jax.random.split(base_key)
    shape_all = (YEARS, DATES, NR, NC)
    chance = jax.random.randint(level_key, shape_all, 0, 1000)
    row_pos = lax.broadcasted_iota(jnp.int32, shape_all, 2)
    year_pos = lax.broadcasted_iota(jnp.int32, shape_all, 0)
    threshold = 250 + 600 * row_pos // max(NR - 1, 1) + 50 * year_pos // max(YEARS - 1, 1)
    others = jax.random.randint(other_key, shape_all, 1, 4)
    return jnp.where(chance < threshold, 0, others).astype(jnp.int32)


def draw_params(key, part):
    base_key = jax.random.fold_in(key, 23)
    lower = jnp.array([0.0, 0.3, -0.3, 0.25, 2.3, 0.6, 2.3], jnp.float32)
    upper = jnp.array([0.2, 0.7, 0.3, 0.45, 3.4, 0.8, 3.4], jnp.float32)
    unit = jax.random.uniform(base_key, (YEARS, PARAMS, NR, NC), jnp.float32)
    return lower[None, :, None, None] + (upper - lower)[None, :, None, None] * unit


def touch_ends(result, own_key, smallest, largest):
    longest = result.shape.index(max(result.shape))
    spots = []
    for shift in (0, 1):
        where = [jax.random.randint(jax.random.fold_in(own_key, axis), (), 0, length) for axis, length in enumerate(result.shape)]
        where[longest] = (where[longest] + shift) % result.shape[longest]
        spots.append(tuple(where))
    return result.at[spots[0]].set(smallest).at[spots[1]].set(largest)


def shard_levels(stream_key, dims, shards, low, top_value):
    loudness = 1.0
    for dim, parts in shards:
        draws = jax.random.uniform(jax.random.fold_in(jax.random.fold_in(stream_key, 6), dim), (parts,), jnp.float32, low / len(shards), top_value / len(shards))
        loudness = loudness * jnp.repeat(jnp.exp(draws), dims[dim] // parts).reshape((-1,) + (1,) * (len(dims) - 1 - dim))
    return loudness


def setup_inputs(seed: int = 0) -> dict:
    key_list = jax.random.split(jax.random.key(seed), 7)
    observed = jnp.clip(0.8 * jax.random.uniform(key_list[0], (YEARS, DATES, NR, NC), jnp.float32) ** shard_levels(key_list[0], (YEARS, DATES, NR, NC), ((0, 4), (2, 2), (3, 4)), -0.2, 0.2), 0.0, 0.8)
    quality = draw_quality(jax.random.fold_in(key_list[6], 71), 0)
    land_mask = touch_ends((jax.random.randint(key_list[2], (NR, NC), 0, 4) < 3).astype(jnp.int32), jax.random.fold_in(key_list[2], 1), 0, 1)
    params = draw_params(jax.random.fold_in(key_list[6], 71), 0)
    spatial_weight = jnp.clip(jnp.exp(jax.random.uniform(key_list[4], (PARAMS,), jnp.float32, math.log(0.2), math.log(2.0))), 0.2, 2.0)
    temporal_weight = jnp.clip(jnp.exp(jax.random.uniform(key_list[5], (PARAMS,), jnp.float32, math.log(0.2), math.log(2.0))), 0.2, 2.0)
    return {"observed": observed, "quality": quality, "land_mask": land_mask, "params": params, "spatial_weight": spatial_weight, "temporal_weight": temporal_weight}


damping = 0.1


def upper_pairs(count):
    return [(left_index, right_index) for left_index in range(count) for right_index in range(left_index, count)]


def curve_terms(observed, quality, land_mask, params):
    num_dates = observed.shape[1]
    count = params.shape[1]
    weight = jnp.where(quality == 0, 1.0, 0.0) + jnp.where(quality == 1, 0.5, 0.0)
    weight = weight * land_mask.astype(jnp.float32)[None, None] / num_dates
    date_times = (jnp.arange(num_dates, dtype=jnp.float32) / num_dates).reshape(1, num_dates, 1, 1)
    level_base, peak_value, green_slope, rise_mid, rise_log, fall_mid, fall_log = [params[:, index][:, None] for index in range(count)]
    rise_rate = jnp.exp(rise_log)
    fall_rate = jnp.exp(fall_log)
    rise_curve = jax.nn.sigmoid(rise_rate * (date_times - rise_mid))
    fall_curve = jax.nn.sigmoid(fall_rate * (date_times - fall_mid))
    season = rise_curve - fall_curve
    amplitude = peak_value - green_slope * date_times
    misfit = level_base + amplitude * season - observed
    rise_slope = rise_curve * (1.0 - rise_curve)
    fall_slope = fall_curve * (1.0 - fall_curve)
    jacobian = [jnp.ones_like(misfit), season, -date_times * season,
                -amplitude * rise_rate * rise_slope,
                amplitude * rise_slope * (date_times - rise_mid) * rise_rate,
                amplitude * fall_rate * fall_slope,
                -amplitude * fall_slope * (date_times - fall_mid) * fall_rate]
    weighted = [weight * column for column in jacobian]
    hessian = jnp.stack([jnp.sum(weighted[left_index] * jacobian[right_index], axis=1) for left_index, right_index in upper_pairs(count)])
    gradient = jnp.stack([jnp.sum(weighted[index] * misfit, axis=1) for index in range(count)], axis=1)
    return hessian, gradient


def blocks_from(hessian, count):
    blocks = [[None] * count for index in range(count)]
    for position, (left_index, right_index) in enumerate(upper_pairs(count)):
        blocks[left_index][right_index] = hessian[position]
        blocks[right_index][left_index] = hessian[position]
    return blocks


def block_apply(blocks, field):
    count = len(blocks)
    outputs = []
    for left_index in range(count):
        total = blocks[left_index][0] * field[:, 0]
        for right_index in range(1, count):
            total = total + blocks[left_index][right_index] * field[:, right_index]
        outputs.append(total)
    return jnp.stack(outputs, axis=1)


def invert(blocks):
    count = len(blocks)
    left_rows = [list(row) for row in blocks]
    right_rows = [[jnp.full_like(blocks[0][0], 1.0 if left_index == right_index else 0.0) for right_index in range(count)] for left_index in range(count)]
    for pivot in range(count):
        scale = 1.0 / left_rows[pivot][pivot]
        left_rows[pivot] = [entry * scale for entry in left_rows[pivot]]
        right_rows[pivot] = [entry * scale for entry in right_rows[pivot]]
        for other in range(count):
            if other != pivot:
                factor = left_rows[other][pivot]
                left_rows[other] = [entry - factor * base_entry for entry, base_entry in zip(left_rows[other], left_rows[pivot])]
                right_rows[other] = [entry - factor * base_entry for entry, base_entry in zip(right_rows[other], right_rows[pivot])]
    return right_rows


def prior_apply(field, spatial_weight, temporal_weight):
    padded = jnp.pad(field, ((1, 1), (0, 0), (1, 1), (1, 1)), mode="edge")
    plane = 4.0 * field - (padded[1:-1, :, :-2, 1:-1] + padded[1:-1, :, 2:, 1:-1] + padded[1:-1, :, 1:-1, :-2] + padded[1:-1, :, 1:-1, 2:])
    yearly = 2.0 * field - (padded[:-2, :, 1:-1, 1:-1] + padded[2:, :, 1:-1, 1:-1])
    return spatial_weight[None, :, None, None] * plane + temporal_weight[None, :, None, None] * yearly


def reference(observed, quality, land_mask, params, spatial_weight, temporal_weight):
    count = params.shape[1]

    def per_year(inputs):
        return curve_terms(inputs[0][None], inputs[1][None], land_mask, inputs[2][None])

    hess_all, grad_all = lax.map(per_year, (observed, quality, params))
    hessian = jnp.moveaxis(hess_all[:, :, 0], 0, 1)
    data_grad = grad_all[:, 0]
    blocks = blocks_from(hessian, count)
    shifted = [list(row) for row in blocks]
    for index in range(count):
        shifted[index][index] = blocks[index][index] + (damping + 4.0 * spatial_weight[index] + 2.0 * temporal_weight[index])
    precond = invert(shifted)

    def operate(field):
        return block_apply(blocks, field) + damping * field + prior_apply(field, spatial_weight, temporal_weight)

    residual = -(data_grad + prior_apply(params, spatial_weight, temporal_weight))
    step_field = jnp.zeros_like(params)
    search = block_apply(precond, residual)
    direction = search
    inner_now = jnp.sum(residual * search)
    for sweep in range(ITERS):
        image = operate(direction)
        step_len = inner_now / jnp.sum(direction * image)
        step_field = step_field + step_len * direction
        residual = residual - step_len * image
        if sweep + 1 < ITERS:
            search = block_apply(precond, residual)
            inner_next = jnp.sum(residual * search)
            direction = search + (inner_next / inner_now) * direction
            inner_now = inner_next
    return params + step_field, residual
```

```python
import functools

import jax
import jax.numpy as jnp
from jax import lax
from jax.experimental import pallas as pl
from jax.experimental.pallas import tpu as pltpu
from jax.sharding import PartitionSpec as P

ITERS = 4
ROUNDS = ITERS + 1
SUB = 8
BLOCKS = 2
DAMPING = 0.1
MESH = pl.DeviceIdType.MESH


def pairs_of(count):
    return [(i, j) for i in range(count) for j in range(i, count)]


def kernel(
    sizes,
    observed,
    quality,
    land,
    params,
    spatial,
    temporal,
    new_params,
    residual,
    obs,
    qual,
    field,
    inverse,
    resid,
    moments,
    plane_slots,
    year_slots,
    load_sem,
    send_sem,
    recv_sem,
    row_send,
    row_recv,
    plane_send,
    plane_recv,
    line_send,
    line_recv,
):
    n_year, n_row, n_col = sizes
    dates, rows, cols = obs.shape
    count = resid.shape[1]
    step_rows = SUB * BLOCKS
    chunks = rows // step_rows
    pairs = pairs_of(count)
    place = {pair: at for at, pair in enumerate(pairs)}

    year, row, col = lax.axis_index("year"), lax.axis_index("row"), lax.axis_index("col")
    even = lax.rem(row, 2) == 0

    has_prev, has_next = year > 0, year < n_year - 1
    has_left, has_right = col > 0, col < n_col - 1
    has_up, has_down = row > 0, row < n_row - 1
    has_first = jnp.logical_or(jnp.logical_and(even, has_up), jnp.logical_and(~even, has_down))
    has_last = jnp.logical_or(jnp.logical_and(even, has_down), jnp.logical_and(~even, has_up))
    toward_first = row + jnp.where(even, -1, 1)
    toward_last = row + jnp.where(even, 1, -1)

    def chunk_rows(position):
        chunk = jnp.where(even, position, chunks - 1 - position)
        return pl.multiple_of(chunk * step_rows, step_rows)

    param_load = pltpu.make_async_copy(
        params.at[0], field.at[0, 0, :, pl.ds(SUB, rows), :], load_sem.at[0]
    )
    param_load.start()

    def input_loads(position):
        start = chunk_rows(position)
        where = (slice(None), pl.ds(start, step_rows), slice(None))
        return (
            pltpu.make_async_copy(observed.at[0].at[where], obs.at[where], load_sem.at[1 + 2 * position]),
            pltpu.make_async_copy(quality.at[0].at[where], qual.at[where], load_sem.at[2 + 2 * position]),
        )

    for position in range(chunks):
        for copy in input_loads(position):
            copy.start()

    barrier = pltpu.get_barrier_semaphore()
    for other in range(1, n_row * n_col):
        spot = lax.rem(row * n_col + col + other, n_row * n_col)
        pl.semaphore_signal(
            barrier, inc=1, device_id=(year, spot // n_col, lax.rem(spot, n_col)), device_id_type=MESH
        )
    for other in range(1, n_year):
        pl.semaphore_signal(
            barrier, inc=1, device_id=(lax.rem(year + other, n_year), row, col), device_id_type=MESH
        )
    pl.semaphore_wait(barrier, n_row * n_col + n_year - 2)

    sides = (
        (has_next, (year + 1, row, col), 1, has_prev),
        (has_prev, (year - 1, row, col), 2, has_next),
        (has_right, (year, row, col + 1), 3, has_left),
        (has_left, (year, row, col - 1), 4, has_right),
    )

    def side_copy(step, position, side):
        _, target, slot, _ = sides[side]
        where = pl.ds(chunk_rows(position) + SUB, step_rows)
        return pltpu.make_async_remote_copy(
            src_ref=field.at[step, 0, :, where, :],
            dst_ref=field.at[step, slot, :, where, :],
            send_sem=send_sem.at[step, side, position],
            recv_sem=recv_sem.at[step, side, position],
            device_id=target,
            device_id_type=MESH,
        )

    def row_copy(step, last):
        top = jnp.logical_xor(even, last)
        source = pl.multiple_of(jnp.where(top, SUB, rows), SUB)
        target = pl.multiple_of(jnp.where(top, rows + SUB, 0), SUB)
        return pltpu.make_async_remote_copy(
            src_ref=field.at[step, 0, :, pl.ds(source, SUB), :],
            dst_ref=field.at[step, 0, :, pl.ds(target, SUB), :],
            send_sem=row_send.at[step, int(last)],
            recv_sem=row_recv.at[step, int(last)],
            device_id=(year, toward_last if last else toward_first, col),
            device_id_type=MESH,
        )

    def start_sends(step, position):
        for side in range(4):
            @pl.when(sides[side][0])
            def _(side=side):
                side_copy(step, position, side).start()

    def wait_sides(step, position):
        for side in range(4):
            @pl.when(sides[side][3])
            def _(side=side):
                side_copy(step, position, side).wait_recv()

    def close_edges(step, first, last):
        for flag, at_last, present in ((first, False, has_first), (last, True, has_last)):
            top = jnp.logical_xor(even, at_last)

            @pl.when(jnp.logical_and(flag, present))
            def _(at_last=at_last):
                row_copy(step, at_last).start()

            def repeat(source, edge, target):
                for p in range(count):
                    block = field[step, 0, p, source : source + SUB, :]
                    field[step, 0, p, target : target + SUB, :] = jnp.broadcast_to(
                        block[edge : edge + 1, :], (SUB, cols)
                    )

            @pl.when(jnp.logical_and(jnp.logical_and(flag, ~present), top))
            def _():
                repeat(SUB, 0, 0)

            @pl.when(jnp.logical_and(jnp.logical_and(flag, ~present), ~top))
            def _():
                repeat(rows, SUB - 1, rows + SUB)

    def wait_edges(step, first, last):
        for flag, at_last, present in ((first, False, has_first), (last, True, has_last)):
            @pl.when(jnp.logical_and(flag, present))
            def _(at_last=at_last):
                row_copy(step, at_last).wait_recv()

    param_load.wait()

    def send_params(position, carry):
        start_sends(0, position)
        return carry

    lax.fori_loop(0, chunks, send_params, 0)
    close_edges(0, True, True)

    prev_slot = jnp.where(has_prev, 1, 0)
    next_slot = jnp.where(has_next, 2, 0)
    left_slot = jnp.where(has_left, 3, 0)
    right_slot = jnp.where(has_right, 4, 0)
    lane = lax.broadcasted_iota(jnp.int32, (SUB, cols), 1)
    level = lax.broadcasted_iota(jnp.int32, (SUB, cols), 0)
    lane_first, lane_last = lane == 0, lane == cols - 1
    level_first, level_last = level == 0, level == SUB - 1
    grid_left = lane == jnp.where(has_left, -1, 0)
    grid_right = lane == jnp.where(has_right, -1, cols - 1)

    def around(step, p, start):
        own = pl.ds(start + SUB, SUB)
        here = field[step, 0, p, own, :]
        above = field[step, 0, p, pl.ds(start, SUB), :]
        below = field[step, 0, p, pl.ds(start + 2 * SUB, SUB), :]
        up = pltpu.roll(jnp.where(level_last, above, here), 1, 0)
        down = pltpu.roll(jnp.where(level_first, below, here), SUB - 1, 0)
        left = pltpu.roll(jnp.where(lane_last, field[step, left_slot, p, own, :], here), 1, 1)
        right = pltpu.roll(
            jnp.where(lane_first, field[step, right_slot, p, own, :], here), cols - 1, 1
        )
        left = jnp.where(grid_left, here, left)
        right = jnp.where(grid_right, here, right)
        plane = (up + down) + (left + right)
        yearly = field[step, prev_slot, p, own, :] + field[step, next_slot, p, own, :]
        return here, spatial[p] * plane + temporal[p] * yearly

    def precondition(start, values):
        rows_here = pl.ds(start, SUB)
        entry = [inverse[at, rows_here, :] for at in range(len(pairs))]
        outs = []
        for p in range(count):
            total = entry[place[(0, p)]] * values[0]
            for q in range(1, count):
                total = total + entry[place[(min(p, q), max(p, q))]] * values[q]
            outs.append(total)
        return outs

    def dot(left, right):
        terms = [a * b for a, b in zip(left, right)]
        while len(terms) > 1:
            terms = [sum(terms[i : i + 2][1:], terms[i]) for i in range(0, len(terms), 2)]
        return terms[0]

    def normal(start):
        here = pl.ds(start, SUB)
        base, peak, slope, rise_mid, rise_log, fall_mid, fall_log = [
            field[0, 0, p, pl.ds(start + SUB, SUB), :] for p in range(count)
        ]
        rise_rate, fall_rate = jnp.exp(rise_log), jnp.exp(fall_log)
        rise_half, fall_half = 0.5 * rise_rate, 0.5 * fall_rate

        def date_step(date, sums):
            time = date.astype(jnp.float32) * (1.0 / dates)
            flag = qual[date, here, :].astype(jnp.float32)
            weight = jnp.maximum(1.0 - 0.5 * flag, 0.0)
            rise_gap = time - rise_mid
            fall_gap = time - fall_mid
            rise = jnp.tanh(rise_half * rise_gap)
            fall = jnp.tanh(fall_half * fall_gap)
            season = rise - fall
            height = peak - slope * time
            rise_bell = height - height * (rise * rise)
            fall_bell = height - height * (fall * fall)
            basis = [
                None,
                season,
                time * season,
                rise_bell,
                rise_gap * rise_bell,
                fall_bell,
                fall_gap * fall_bell,
            ]
            weighted = [weight] + [weight * item for item in basis[1:]]
            out = []
            for i, j in pairs:
                term = weighted[j] if i == 0 else basis[i] * weighted[j]
                out.append(sums[place[(i, j)]] + term)
            seen = obs[date, here, :]
            for i in range(count):
                out.append(sums[len(pairs) + i] + seen * weighted[i])
            return tuple(out)

        zero = jnp.zeros((SUB, cols), jnp.float32)
        sums = lax.fori_loop(
            0, dates, date_step, (zero,) * (len(pairs) + count), unroll=2
        )
        share = land[here, :].astype(jnp.float32) * (1.0 / dates)
        rise_scale, fall_scale = 0.25 * rise_rate, 0.25 * fall_rate
        scale = [None, 0.5, -0.5, -rise_scale, rise_scale, fall_scale, -fall_scale]
        shared = [share] + [share * item for item in scale[1:]]
        block = {}
        for i, j in pairs:
            factor = shared[j] if i == 0 else shared[j] * scale[i]
            block[(i, j)] = sums[place[(i, j)]] * factor
        for p in range(count):
            total = shared[p] * sums[len(pairs) + p]
            for q, value in ((0, base), (1, peak), (2, slope)):
                total = total - block[(min(p, q), max(p, q))] * value
            resid[0, p, here, :] = total
        for p in range(count):
            block[(p, p)] = block[(p, p)] + (DAMPING + 4.0 * spatial[p] + 2.0 * temporal[p])
        for k in range(count):
            turn = 1.0 / block[(k, k)]
            edge = {i: block[(min(i, k), max(i, k))] for i in range(count) if i != k}
            lean = {i: edge[i] * turn for i in edge}
            for i, j in pairs:
                if i != k and j != k:
                    block[(i, j)] = block[(i, j)] - edge[i] * lean[j]
            for i in edge:
                block[(min(i, k), max(i, k))] = lean[i]
            block[(k, k)] = -turn
        for pair in pairs:
            inverse[place[pair], here, :] = -block[pair]

    zero = jnp.zeros((SUB, cols), jnp.float32)

    def make_stage(stage):
        def body(position, carry):
            odd_sum, even_sum = carry
            start = chunk_rows(position)
            first, last = position == 0, position == chunks - 1
            if stage == 0:
                for copy in input_loads(position):
                    copy.wait()

                def each(b, c):
                    normal(pl.multiple_of(start + b * SUB, SUB))
                    return c

                lax.fori_loop(0, BLOCKS, each, 0)
            before = stage
            wait_sides(before, position)
            wait_edges(before, first, last)
            for b in range(BLOCKS):
                at = pl.multiple_of(start + b * SUB, SUB)
                rows_here = pl.ds(at, SUB)
                held, pushed = [], []
                for p in range(count):
                    here, push = around(before, p, at)
                    if stage == 0:
                        push = (resid[0, p, rows_here, :] + push) - (
                            4.0 * spatial[p] + 2.0 * temporal[p]
                        ) * here
                    resid[stage, p, rows_here, :] = push
                    held.append(here)
                    pushed.append(push)
                if stage > 0:
                    odd_sum = odd_sum + dot(held, pushed)
                if stage < ITERS:
                    turned = precondition(at, pushed)
                    for p in range(count):
                        field[stage + 1, 0, p, pl.ds(at + SUB, SUB), :] = turned[p]
                    even_sum = even_sum + dot(turned, pushed)
            if stage < ITERS:
                start_sends(stage + 1, position)
                close_edges(stage + 1, first, last)
            return odd_sum, even_sum

        return body

    sums = []
    for stage in range(ITERS + 1):
        odd_sum, even_sum = lax.fori_loop(0, chunks, make_stage(stage), (zero, zero))
        if stage > 0:
            sums.append(odd_sum)
        if stage < ITERS:
            sums.append(even_sum)

    for at, value in enumerate(sums):
        moments[0, at : at + 1, :] = jnp.sum(value, axis=0, keepdims=True)

    def plane_copy(other):
        spot = lax.rem(row * n_col + col + other, n_row * n_col)
        return pltpu.make_async_remote_copy(
            src_ref=moments.at[0],
            dst_ref=plane_slots.at[other - 1],
            send_sem=plane_send.at[other - 1],
            recv_sem=plane_recv.at[other - 1],
            device_id=(year, spot // n_col, lax.rem(spot, n_col)),
            device_id_type=MESH,
        )

    def line_copy(other):
        return pltpu.make_async_remote_copy(
            src_ref=moments.at[1],
            dst_ref=year_slots.at[other - 1],
            send_sem=line_send.at[other - 1],
            recv_sem=line_recv.at[other - 1],
            device_id=(lax.rem(year + other, n_year), row, col),
            device_id_type=MESH,
        )

    for other in range(1, n_row * n_col):
        plane_copy(other).start()
    total = moments[0]
    for other in range(1, n_row * n_col):
        plane_copy(other).wait_recv()
        total = total + plane_slots[other - 1]
    moments[1] = total
    for other in range(1, n_year):
        line_copy(other).start()
    for other in range(1, n_year):
        line_copy(other).wait_recv()
        total = total + year_slots[other - 1]
    total = jnp.broadcast_to(jnp.sum(total, axis=1, keepdims=True), total.shape)
    mu = [total[at : at + 1, :] for at in range(2 * ITERS)]
    drop = [mu[at] - mu[at + 1] for at in range(2 * ITERS - 1)]

    def form(coefs, table):
        total = None
        for i, left in enumerate(coefs):
            for j in range(i, len(coefs)):
                term = left * coefs[j] * table[i + j]
                term = term if i == j else 2.0 * term
                total = term if total is None else total + term
        return total

    one = jnp.ones_like(mu[0])
    search, direction = [one], [one]
    lengths = [jnp.zeros_like(one)] * ITERS
    inner = mu[0]
    for sweep in range(ITERS):
        alpha = inner / form(direction, drop)
        for j in range(sweep + 1):
            lengths[j] = lengths[j] + alpha * direction[j]
        if sweep + 1 < ITERS:
            grown = []
            for j in range(sweep + 2):
                change = None
                if j <= sweep:
                    change = direction[j]
                if j > 0:
                    change = -direction[j - 1] if change is None else change - direction[j - 1]
                base = search[j] if j <= sweep else None
                grown.append(-alpha * change if base is None else base - alpha * change)
            search = grown
            fresh = form(search, mu)
            ratio = fresh / inner
            inner = fresh
            direction = [
                search[j] + ratio * direction[j] if j <= sweep else search[j]
                for j in range(sweep + 2)
            ]

    steps = [jnp.broadcast_to(value, (SUB, cols)) for value in lengths]
    mixes = [1.0 - steps[0]]
    mixes += [steps[j - 1] - steps[j] for j in range(1, ITERS)]
    mixes += [steps[-1]]

    def finish(b, carry):
        at = pl.multiple_of(b * SUB, SUB)
        rows_here = pl.ds(at, SUB)
        padded = pl.ds(at + SUB, SUB)
        for p in range(count):
            total = field[0, 0, p, padded, :]
            for j in range(ITERS):
                total = total + steps[j] * field[j + 1, 0, p, padded, :]
            new_params[0, p, rows_here, :] = total
            total = mixes[0] * resid[0, p, rows_here, :]
            for j in range(1, ITERS + 1):
                total = total + mixes[j] * resid[j, p, rows_here, :]
            residual[0, p, rows_here, :] = total
        return carry

    lax.fori_loop(0, rows // SUB, finish, 0)

    for step in range(ROUNDS):
        def drain(position, carry, step=step):
            for side in range(4):
                @pl.when(sides[side][0])
                def _(side=side):
                    side_copy(step, position, side).wait_send()
            return carry

        lax.fori_loop(0, chunks, drain, 0)
        for at_last, present in ((False, has_first), (True, has_last)):
            @pl.when(present)
            def _(at_last=at_last, step=step):
                row_copy(step, at_last).wait_send()
    for other in range(1, n_row * n_col):
        plane_copy(other).wait_send()
    for other in range(1, n_year):
        line_copy(other).wait_send()


def per_device(sizes, observed, quality, land_mask, params, spatial_weight, temporal_weight):
    n_year, n_row, n_col = sizes
    _, dates, rows, cols = observed.shape
    count = params.shape[1]
    chunks = rows // (SUB * BLOCKS)
    f32 = jnp.float32
    vmem = pl.BlockSpec(memory_space=pltpu.VMEM)
    hbm = pl.BlockSpec(memory_space=pltpu.HBM)
    smem = pl.BlockSpec(memory_space=pltpu.SMEM)
    dma = pltpu.SemaphoreType.DMA
    return pl.pallas_call(
        functools.partial(kernel, sizes),
        out_shape=(
            jax.ShapeDtypeStruct(params.shape, f32),
            jax.ShapeDtypeStruct(params.shape, f32),
        ),
        in_specs=[hbm, hbm, vmem, hbm, smem, smem],
        out_specs=(vmem, vmem),
        scratch_shapes=[
            pltpu.VMEM((dates, rows, cols), f32),
            pltpu.VMEM((dates, rows, cols), jnp.int32),
            pltpu.VMEM((ROUNDS, 5, count, rows + 2 * SUB, cols), f32),
            pltpu.VMEM((count * (count + 1) // 2, rows, cols), f32),
            pltpu.VMEM((ROUNDS, count, rows, cols), f32),
            pltpu.VMEM((2, 2 * ITERS, cols), f32),
            pltpu.VMEM((max(n_row * n_col - 1, 1), 2 * ITERS, cols), f32),
            pltpu.VMEM((max(n_year - 1, 1), 2 * ITERS, cols), f32),
            dma((1 + 2 * chunks,)),
            dma((ROUNDS, 4, chunks)),
            dma((ROUNDS, 4, chunks)),
            dma((ROUNDS, 2)),
            dma((ROUNDS, 2)),
            dma((max(n_row * n_col - 1, 1),)),
            dma((max(n_row * n_col - 1, 1),)),
            dma((max(n_year - 1, 1),)),
            dma((max(n_year - 1, 1),)),
        ],
        compiler_params=pltpu.CompilerParams(
            collective_id=0, has_side_effects=True, vmem_limit_bytes=48 * 1024 * 1024
        ),
        name="gauss_newton",
    )(observed, quality, land_mask, params, spatial_weight, temporal_weight)


def solution(mesh):
    sizes = tuple(mesh.shape[axis] for axis in ("year", "row", "col"))
    grid = P("year", None, "row", "col")
    return jax.shard_map(
        functools.partial(per_device, sizes),
        mesh=mesh,
        in_specs=(grid, grid, P("row", "col"), grid, P(), P()),
        out_specs=(grid, grid),
        check_vma=False,
    )
```

```python
import functools

import jax
import jax.numpy as jnp
from jax import lax
from jax.experimental import pallas as pl
from jax.experimental.pallas import tpu as pltpu
from jax.sharding import PartitionSpec as P

ITERS = 4
ROUNDS = ITERS + 1
SUB = 8
BLOCKS = 2
DAMPING = 0.1
MESH = pl.DeviceIdType.MESH


def pairs_of(count):
    return [(i, j) for i in range(count) for j in range(i, count)]


def kernel(
    sizes,
    observed,
    quality,
    land,
    params,
    spatial,
    temporal,
    new_params,
    residual,
    obs,
    qual,
    field,
    inverse,
    resid,
    moments,
    plane_slots,
    year_slots,
    load_sem,
    send_sem,
    recv_sem,
    row_send,
    row_recv,
    plane_send,
    plane_recv,
    line_send,
    line_recv,
):
    n_year, n_row, n_col = sizes
    dates, rows, cols = obs.shape
    count = resid.shape[1]
    step_rows = SUB * BLOCKS
    chunks = rows // step_rows
    pairs = pairs_of(count)
    place = {pair: at for at, pair in enumerate(pairs)}

    year, row, col = lax.axis_index("year"), lax.axis_index("row"), lax.axis_index("col")
    even = lax.rem(row, 2) == 0

    has_prev, has_next = year > 0, year < n_year - 1
    has_left, has_right = col > 0, col < n_col - 1
    has_up, has_down = row > 0, row < n_row - 1
    has_first = jnp.logical_or(jnp.logical_and(even, has_up), jnp.logical_and(~even, has_down))
    has_last = jnp.logical_or(jnp.logical_and(even, has_down), jnp.logical_and(~even, has_up))
    toward_first = row + jnp.where(even, -1, 1)
    toward_last = row + jnp.where(even, 1, -1)

    def chunk_rows(position):
        chunk = jnp.where(even, position, chunks - 1 - position)
        return pl.multiple_of(chunk * step_rows, step_rows)

    param_load = pltpu.make_async_copy(
        params.at[0], field.at[0, 0, :, pl.ds(SUB, rows), :], load_sem.at[0]
    )
    param_load.start()

    def input_loads(position):
        start = chunk_rows(position)
        where = (slice(None), pl.ds(start, step_rows), slice(None))
        return (
            pltpu.make_async_copy(observed.at[0].at[where], obs.at[where], load_sem.at[1 + 2 * position]),
            pltpu.make_async_copy(quality.at[0].at[where], qual.at[where], load_sem.at[2 + 2 * position]),
        )

    for position in range(chunks):
        for copy in input_loads(position):
            copy.start()

    barrier = pltpu.get_barrier_semaphore()
    for other in range(1, n_row * n_col):
        spot = lax.rem(row * n_col + col + other, n_row * n_col)
        pl.semaphore_signal(
            barrier, inc=1, device_id=(year, spot // n_col, lax.rem(spot, n_col)), device_id_type=MESH
        )
    for other in range(1, n_year):
        pl.semaphore_signal(
            barrier, inc=1, device_id=(lax.rem(year + other, n_year), row, col), device_id_type=MESH
        )
    pl.semaphore_wait(barrier, n_row * n_col + n_year - 2)

    sides = (
        (has_next, (year + 1, row, col), 1, has_prev),
        (has_prev, (year - 1, row, col), 2, has_next),
        (has_right, (year, row, col + 1), 3, has_left),
        (has_left, (year, row, col - 1), 4, has_right),
    )

    def side_copy(step, position, side):
        _, target, slot, _ = sides[side]
        where = pl.ds(chunk_rows(position) + SUB, step_rows)
        return pltpu.make_async_remote_copy(
            src_ref=field.at[step, 0, :, where, :],
            dst_ref=field.at[step, slot, :, where, :],
            send_sem=send_sem.at[step, side, position],
            recv_sem=recv_sem.at[step, side, position],
            device_id=target,
            device_id_type=MESH,
        )

    def row_copy(step, last):
        top = jnp.logical_xor(even, last)
        source = pl.multiple_of(jnp.where(top, SUB, rows), SUB)
        target = pl.multiple_of(jnp.where(top, rows + SUB, 0), SUB)
        return pltpu.make_async_remote_copy(
            src_ref=field.at[step, 0, :, pl.ds(source, SUB), :],
            dst_ref=field.at[step, 0, :, pl.ds(target, SUB), :],
            send_sem=row_send.at[step, int(last)],
            recv_sem=row_recv.at[step, int(last)],
            device_id=(year, toward_last if last else toward_first, col),
            device_id_type=MESH,
        )

    def start_sends(step, position):
        for side in range(4):
            @pl.when(sides[side][0])
            def _(side=side):
                side_copy(step, position, side).start()

    def wait_sides(step, position):
        for side in range(4):
            @pl.when(sides[side][3])
            def _(side=side):
                side_copy(step, position, side).wait_recv()

    def close_edges(step, first, last):
        for flag, at_last, present in ((first, False, has_first), (last, True, has_last)):
            top = jnp.logical_xor(even, at_last)

            @pl.when(jnp.logical_and(flag, present))
            def _(at_last=at_last):
                row_copy(step, at_last).start()

            def repeat(source, edge, target):
                for p in range(count):
                    block = field[step, 0, p, source : source + SUB, :]
                    field[step, 0, p, target : target + SUB, :] = jnp.broadcast_to(
                        block[edge : edge + 1, :], (SUB, cols)
                    )

            @pl.when(jnp.logical_and(jnp.logical_and(flag, ~present), top))
            def _():
                repeat(SUB, 0, 0)

            @pl.when(jnp.logical_and(jnp.logical_and(flag, ~present), ~top))
            def _():
                repeat(rows, SUB - 1, rows + SUB)

    def wait_edges(step, first, last):
        for flag, at_last, present in ((first, False, has_first), (last, True, has_last)):
            @pl.when(jnp.logical_and(flag, present))
            def _(at_last=at_last):
                row_copy(step, at_last).wait_recv()

    param_load.wait()

    def send_params(position, carry):
        start_sends(0, position)
        return carry

    lax.fori_loop(0, chunks, send_params, 0)
    close_edges(0, True, True)

    prev_slot = jnp.where(has_prev, 1, 0)
    next_slot = jnp.where(has_next, 2, 0)
    left_slot = jnp.where(has_left, 3, 0)
    right_slot = jnp.where(has_right, 4, 0)
    lane = lax.broadcasted_iota(jnp.int32, (SUB, cols), 1)
    level = lax.broadcasted_iota(jnp.int32, (SUB, cols), 0)
    lane_first, lane_last = lane == 0, lane == cols - 1
    level_first, level_last = level == 0, level == SUB - 1
    grid_left = lane == jnp.where(has_left, -1, 0)
    grid_right = lane == jnp.where(has_right, -1, cols - 1)

    def around(step, p, start):
        own = pl.ds(start + SUB, SUB)
        here = field[step, 0, p, own, :]
        above = field[step, 0, p, pl.ds(start, SUB), :]
        below = field[step, 0, p, pl.ds(start + 2 * SUB, SUB), :]
        up = pltpu.roll(jnp.where(level_last, above, here), 1, 0)
        down = pltpu.roll(jnp.where(level_first, below, here), SUB - 1, 0)
        left = pltpu.roll(jnp.where(lane_last, field[step, left_slot, p, own, :], here), 1, 1)
        right = pltpu.roll(
            jnp.where(lane_first, field[step, right_slot, p, own, :], here), cols - 1, 1
        )
        left = jnp.where(grid_left, here, left)
        right = jnp.where(grid_right, here, right)
        plane = (up + down) + (left + right)
        yearly = field[step, prev_slot, p, own, :] + field[step, next_slot, p, own, :]
        return here, spatial[p] * plane + temporal[p] * yearly

    def precondition(start, values):
        rows_here = pl.ds(start, SUB)
        entry = [inverse[at, rows_here, :] for at in range(len(pairs))]
        outs = []
        for p in range(count):
            total = entry[place[(0, p)]] * values[0]
            for q in range(1, count):
                total = total + entry[place[(min(p, q), max(p, q))]] * values[q]
            outs.append(total)
        return outs

    def dot(left, right):
        terms = [a * b for a, b in zip(left, right)]
        while len(terms) > 1:
            terms = [sum(terms[i : i + 2][1:], terms[i]) for i in range(0, len(terms), 2)]
        return terms[0]

    def normal(start):
        here = pl.ds(start, SUB)
        base, peak, slope, rise_mid, rise_log, fall_mid, fall_log = [
            field[0, 0, p, pl.ds(start + SUB, SUB), :] for p in range(count)
        ]
        rise_rate, fall_rate = jnp.exp(rise_log), jnp.exp(fall_log)
        rise_half, fall_half = 0.5 * rise_rate, 0.5 * fall_rate

        def date_step(date, sums):
            time = date.astype(jnp.float32) * (1.0 / dates)
            flag = qual[date, here, :].astype(jnp.float32)
            weight = jnp.maximum(1.0 - 0.5 * flag, 0.0)
            rise_gap = time - rise_mid
            fall_gap = time - fall_mid
            rise = jnp.tanh(rise_half * rise_gap)
            fall = jnp.tanh(fall_half * fall_gap)
            season = rise - fall
            height = peak - slope * time
            rise_bell = height - height * (rise * rise)
            fall_bell = height - height * (fall * fall)
            basis = [
                None,
                season,
                time * season,
                rise_bell,
                rise_gap * rise_bell,
                fall_bell,
                fall_gap * fall_bell,
            ]
            weighted = [weight] + [weight * item for item in basis[1:]]
            out = []
            for i, j in pairs:
                term = weighted[j] if i == 0 else basis[i] * weighted[j]
                out.append(sums[place[(i, j)]] + term)
            seen = obs[date, here, :]
            for i in range(count):
                out.append(sums[len(pairs) + i] + seen * weighted[i])
            return tuple(out)

        zero = jnp.zeros((SUB, cols), jnp.float32)
        sums = lax.fori_loop(
            0, dates, date_step, (zero,) * (len(pairs) + count), unroll=2
        )
        share = land[here, :].astype(jnp.float32) * (1.0 / dates)
        rise_scale, fall_scale = 0.25 * rise_rate, 0.25 * fall_rate
        scale = [None, 0.5, -0.5, -rise_scale, rise_scale, fall_scale, -fall_scale]
        shared = [share] + [share * item for item in scale[1:]]
        block = {}
        for i, j in pairs:
            factor = shared[j] if i == 0 else shared[j] * scale[i]
            block[(i, j)] = sums[place[(i, j)]] * factor
        for p in range(count):
            total = shared[p] * sums[len(pairs) + p]
            for q, value in ((0, base), (1, peak), (2, slope)):
                total = total - block[(min(p, q), max(p, q))] * value
            resid[0, p, here, :] = total
        for p in range(count):
            block[(p, p)] = block[(p, p)] + (DAMPING + 4.0 * spatial[p] + 2.0 * temporal[p])
        for k in range(count):
            turn = 1.0 / block[(k, k)]
            edge = {i: block[(min(i, k), max(i, k))] for i in range(count) if i != k}
            lean = {i: edge[i] * turn for i in edge}
            for i, j in pairs:
                if i != k and j != k:
                    block[(i, j)] = block[(i, j)] - edge[i] * lean[j]
            for i in edge:
                block[(min(i, k), max(i, k))] = lean[i]
            block[(k, k)] = -turn
        for pair in pairs:
            inverse[place[pair], here, :] = -block[pair]

    zero = jnp.zeros((SUB, cols), jnp.float32)

    def make_stage(stage):
        def body(position, carry):
            odd_sum, even_sum = carry
            start = chunk_rows(position)
            first, last = position == 0, position == chunks - 1
            if stage == 0:
                for copy in input_loads(position):
                    copy.wait()

                def each(b, c):
                    normal(pl.multiple_of(start + b * SUB, SUB))
                    return c

                lax.fori_loop(0, BLOCKS, each, 0)
            before = stage
            wait_sides(before, position)
            wait_edges(before, first, last)
            for b in range(BLOCKS):
                at = pl.multiple_of(start + b * SUB, SUB)
                rows_here = pl.ds(at, SUB)
                held, pushed = [], []
                for p in range(count):
                    here, push = around(before, p, at)
                    if stage == 0:
                        push = (resid[0, p, rows_here, :] + push) - (
                            4.0 * spatial[p] + 2.0 * temporal[p]
                        ) * here
                    resid[stage, p, rows_here, :] = push
                    held.append(here)
                    pushed.append(push)
                if stage > 0:
                    odd_sum = odd_sum + dot(held, pushed)
                if stage < ITERS:
                    turned = precondition(at, pushed)
                    for p in range(count):
                        field[stage + 1, 0, p, pl.ds(at + SUB, SUB), :] = turned[p]
                    even_sum = even_sum + dot(turned, pushed)
            if stage < ITERS:
                start_sends(stage + 1, position)
                close_edges(stage + 1, first, last)
            return odd_sum, even_sum

        return body

    sums = []
    for stage in range(ITERS + 1):
        odd_sum, even_sum = lax.fori_loop(0, chunks, make_stage(stage), (zero, zero))
        if stage > 0:
            sums.append(odd_sum)
        if stage < ITERS:
            sums.append(even_sum)

    for at, value in enumerate(sums):
        moments[0, at : at + 1, :] = jnp.sum(value, axis=0, keepdims=True)

    def plane_copy(other):
        spot = lax.rem(row * n_col + col + other, n_row * n_col)
        return pltpu.make_async_remote_copy(
            src_ref=moments.at[0],
            dst_ref=plane_slots.at[other - 1],
            send_sem=plane_send.at[other - 1],
            recv_sem=plane_recv.at[other - 1],
            device_id=(year, spot // n_col, lax.rem(spot, n_col)),
            device_id_type=MESH,
        )

    def line_copy(other):
        return pltpu.make_async_remote_copy(
            src_ref=moments.at[1],
            dst_ref=year_slots.at[other - 1],
            send_sem=line_send.at[other - 1],
            recv_sem=line_recv.at[other - 1],
            device_id=(lax.rem(year + other, n_year), row, col),
            device_id_type=MESH,
        )

    for other in range(1, n_row * n_col):
        plane_copy(other).start()
    total = moments[0]
    for other in range(1, n_row * n_col):
        plane_copy(other).wait_recv()
        total = total + plane_slots[other - 1]
    moments[1] = total
    for other in range(1, n_year):
        line_copy(other).start()
    for other in range(1, n_year):
        line_copy(other).wait_recv()
        total = total + year_slots[other - 1]
    total = jnp.broadcast_to(jnp.sum(total, axis=1, keepdims=True), total.shape)
    mu = [total[at : at + 1, :] for at in range(2 * ITERS)]
    drop = [mu[at] - mu[at + 1] for at in range(2 * ITERS - 1)]

    def form(coefs, table):
        total = None
        for i, left in enumerate(coefs):
            for j in range(i, len(coefs)):
                term = left * coefs[j] * table[i + j]
                term = term if i == j else 2.0 * term
                total = term if total is None else total + term
        return total

    one = jnp.ones_like(mu[0])
    search, direction = [one], [one]
    lengths = [jnp.zeros_like(one)] * ITERS
    inner = mu[0]
    for sweep in range(ITERS):
        alpha = inner / form(direction, drop)
        for j in range(sweep + 1):
            lengths[j] = lengths[j] + alpha * direction[j]
        if sweep + 1 < ITERS:
            grown = []
            for j in range(sweep + 2):
                change = None
                if j <= sweep:
                    change = direction[j]
                if j > 0:
                    change = -direction[j - 1] if change is None else change - direction[j - 1]
                base = search[j] if j <= sweep else None
                grown.append(-alpha * change if base is None else base - alpha * change)
            search = grown
            fresh = form(search, mu)
            ratio = fresh / inner
            inner = fresh
            direction = [
                search[j] + ratio * direction[j] if j <= sweep else search[j]
                for j in range(sweep + 2)
            ]

    steps = [jnp.broadcast_to(value, (SUB, cols)) for value in lengths]
    mixes = [1.0 - steps[0]]
    mixes += [steps[j - 1] - steps[j] for j in range(1, ITERS)]
    mixes += [steps[-1]]

    def finish(b, carry):
        at = pl.multiple_of(b * SUB, SUB)
        rows_here = pl.ds(at, SUB)
        padded = pl.ds(at + SUB, SUB)
        for p in range(count):
            total = field[0, 0, p, padded, :]
            for j in range(ITERS):
                total = total + steps[j] * field[j + 1, 0, p, padded, :]
            new_params[0, p, rows_here, :] = total
            total = mixes[0] * resid[0, p, rows_here, :]
            for j in range(1, ITERS + 1):
                total = total + mixes[j] * resid[j, p, rows_here, :]
            residual[0, p, rows_here, :] = total
        return carry

    lax.fori_loop(0, rows // SUB, finish, 0)

    for step in range(ROUNDS):
        def drain(position, carry, step=step):
            for side in range(4):
                @pl.when(sides[side][0])
                def _(side=side):
                    side_copy(step, position, side).wait_send()
            return carry

        lax.fori_loop(0, chunks, drain, 0)
        for at_last, present in ((False, has_first), (True, has_last)):
            @pl.when(present)
            def _(at_last=at_last, step=step):
                row_copy(step, at_last).wait_send()
    for other in range(1, n_row * n_col):
        plane_copy(other).wait_send()
    for other in range(1, n_year):
        line_copy(other).wait_send()


def per_device(sizes, observed, quality, land_mask, params, spatial_weight, temporal_weight):
    n_year, n_row, n_col = sizes
    _, dates, rows, cols = observed.shape
    count = params.shape[1]
    chunks = rows // (SUB * BLOCKS)
    f32 = jnp.float32
    vmem = pl.BlockSpec(memory_space=pltpu.VMEM)
    hbm = pl.BlockSpec(memory_space=pltpu.HBM)
    smem = pl.BlockSpec(memory_space=pltpu.SMEM)
    dma = pltpu.SemaphoreType.DMA
    return pl.pallas_call(
        functools.partial(kernel, sizes),
        out_shape=(
            jax.ShapeDtypeStruct(params.shape, f32),
            jax.ShapeDtypeStruct(params.shape, f32),
        ),
        in_specs=[hbm, hbm, vmem, hbm, smem, smem],
        out_specs=(vmem, vmem),
        scratch_shapes=[
            pltpu.VMEM((dates, rows, cols), f32),
            pltpu.VMEM((dates, rows, cols), jnp.int32),
            pltpu.VMEM((ROUNDS, 5, count, rows + 2 * SUB, cols), f32),
            pltpu.VMEM((count * (count + 1) // 2, rows, cols), f32),
            pltpu.VMEM((ROUNDS, count, rows, cols), f32),
            pltpu.VMEM((2, 2 * ITERS, cols), f32),
            pltpu.VMEM((max(n_row * n_col - 1, 1), 2 * ITERS, cols), f32),
            pltpu.VMEM((max(n_year - 1, 1), 2 * ITERS, cols), f32),
            dma((1 + 2 * chunks,)),
            dma((ROUNDS, 4, chunks)),
            dma((ROUNDS, 4, chunks)),
            dma((ROUNDS, 2)),
            dma((ROUNDS, 2)),
            dma((max(n_row * n_col - 1, 1),)),
            dma((max(n_row * n_col - 1, 1),)),
            dma((max(n_year - 1, 1),)),
            dma((max(n_year - 1, 1),)),
        ],
        compiler_params=pltpu.CompilerParams(
            collective_id=0, has_side_effects=True, vmem_limit_bytes=67043328
        ),
        name="gauss_newton",
    )(observed, quality, land_mask, params, spatial_weight, temporal_weight)


def solution(mesh):
    sizes = tuple(mesh.shape[axis] for axis in ("year", "row", "col"))
    grid = P("year", None, "row", "col")
    return jax.shard_map(
        functools.partial(per_device, sizes),
        mesh=mesh,
        in_specs=(grid, grid, P("row", "col"), grid, P(), P()),
        out_specs=(grid, grid),
        check_vma=False,
    )
```

```python
import functools

import jax
import jax.numpy as jnp
from jax import lax
from jax.experimental import pallas as pl
from jax.experimental.pallas import tpu as pltpu
from jax.sharding import PartitionSpec as P

ITERS = 4
ROUNDS = ITERS + 1
SUB = 8
BLOCKS = 2
DAMPING = 0.1
MESH = pl.DeviceIdType.MESH


def pairs_of(count):
    return [(i, j) for i in range(count) for j in range(i, count)]


def kernel(
    sizes,
    observed,
    quality,
    land,
    params,
    spatial,
    temporal,
    new_params,
    residual,
    obs,
    qual,
    field,
    inverse,
    resid,
    moments,
    slots,
    load_sem,
    send_sem,
    recv_sem,
    row_send,
    row_recv,
    sum_send,
    sum_recv,
):
    n_year, n_row, n_col = sizes
    dates, rows, cols = obs.shape
    count = resid.shape[1]
    step_rows = SUB * BLOCKS
    chunks = rows // step_rows
    pairs = pairs_of(count)
    place = {pair: at for at, pair in enumerate(pairs)}

    year, row, col = lax.axis_index("year"), lax.axis_index("row"), lax.axis_index("col")
    even = lax.rem(row, 2) == 0

    has_prev, has_next = year > 0, year < n_year - 1
    has_left, has_right = col > 0, col < n_col - 1
    has_up, has_down = row > 0, row < n_row - 1
    has_first = jnp.logical_or(jnp.logical_and(even, has_up), jnp.logical_and(~even, has_down))
    has_last = jnp.logical_or(jnp.logical_and(even, has_down), jnp.logical_and(~even, has_up))
    toward_first = row + jnp.where(even, -1, 1)
    toward_last = row + jnp.where(even, 1, -1)

    def chunk_rows(position):
        chunk = jnp.where(even, position, chunks - 1 - position)
        return pl.multiple_of(chunk * step_rows, step_rows)

    param_load = pltpu.make_async_copy(
        params.at[0], field.at[0, 0, :, pl.ds(SUB, rows), :], load_sem.at[0]
    )
    param_load.start()

    def input_loads(position):
        start = chunk_rows(position)
        where = (slice(None), pl.ds(start, step_rows), slice(None))
        return (
            pltpu.make_async_copy(observed.at[0].at[where], obs.at[where], load_sem.at[1 + 2 * position]),
            pltpu.make_async_copy(quality.at[0].at[where], qual.at[where], load_sem.at[2 + 2 * position]),
        )

    for position in range(chunks):
        for copy in input_loads(position):
            copy.start()

    total_devices = n_year * n_row * n_col
    near = (n_year - 1) + (n_row - 1) <= ITERS

    def peer(other):
        spot = lax.rem((year * n_row + row) * n_col + col + other, total_devices)
        return (spot // (n_row * n_col), lax.rem(spot // n_col, n_row), lax.rem(spot, n_col))

    barrier = pltpu.get_barrier_semaphore()
    if near:
        for other in range(1, n_col):
            pl.semaphore_signal(
                barrier,
                inc=1,
                device_id=(year, row, lax.rem(col + other, n_col)),
                device_id_type=MESH,
            )
        expected = n_col - 1
        for present, target in (
            (has_prev, (year - 1, row, col)),
            (has_next, (year + 1, row, col)),
            (has_up, (year, row - 1, col)),
            (has_down, (year, row + 1, col)),
        ):
            @pl.when(present)
            def _(target=target):
                pl.semaphore_signal(barrier, inc=1, device_id=target, device_id_type=MESH)

            expected = expected + present.astype(jnp.int32)
        pl.semaphore_wait(barrier, expected)
    else:
        for other in range(1, total_devices):
            pl.semaphore_signal(barrier, inc=1, device_id=peer(other), device_id_type=MESH)
        pl.semaphore_wait(barrier, total_devices - 1)

    sides = (
        (has_next, (year + 1, row, col), 1, has_prev),
        (has_prev, (year - 1, row, col), 2, has_next),
        (has_right, (year, row, col + 1), 3, has_left),
        (has_left, (year, row, col - 1), 4, has_right),
    )

    def side_copy(step, position, side):
        _, target, slot, _ = sides[side]
        where = pl.ds(chunk_rows(position) + SUB, step_rows)
        return pltpu.make_async_remote_copy(
            src_ref=field.at[step, 0, :, where, :],
            dst_ref=field.at[step, slot, :, where, :],
            send_sem=send_sem.at[step, side, position],
            recv_sem=recv_sem.at[step, side, position],
            device_id=target,
            device_id_type=MESH,
        )

    def row_copy(step, last):
        top = jnp.logical_xor(even, last)
        source = pl.multiple_of(jnp.where(top, SUB, rows), SUB)
        target = pl.multiple_of(jnp.where(top, rows + SUB, 0), SUB)
        return pltpu.make_async_remote_copy(
            src_ref=field.at[step, 0, :, pl.ds(source, SUB), :],
            dst_ref=field.at[step, 0, :, pl.ds(target, SUB), :],
            send_sem=row_send.at[step, int(last)],
            recv_sem=row_recv.at[step, int(last)],
            device_id=(year, toward_last if last else toward_first, col),
            device_id_type=MESH,
        )

    def start_sends(step, position):
        for side in range(4):
            @pl.when(sides[side][0])
            def _(side=side):
                side_copy(step, position, side).start()

    def wait_sides(step, position):
        for side in range(4):
            @pl.when(sides[side][3])
            def _(side=side):
                side_copy(step, position, side).wait_recv()

    def close_edges(step, first, last):
        for flag, at_last, present in ((first, False, has_first), (last, True, has_last)):
            top = jnp.logical_xor(even, at_last)

            @pl.when(jnp.logical_and(flag, present))
            def _(at_last=at_last):
                row_copy(step, at_last).start()

            def repeat(source, edge, target):
                for p in range(count):
                    block = field[step, 0, p, source : source + SUB, :]
                    field[step, 0, p, target : target + SUB, :] = jnp.broadcast_to(
                        block[edge : edge + 1, :], (SUB, cols)
                    )

            @pl.when(jnp.logical_and(jnp.logical_and(flag, ~present), top))
            def _():
                repeat(SUB, 0, 0)

            @pl.when(jnp.logical_and(jnp.logical_and(flag, ~present), ~top))
            def _():
                repeat(rows, SUB - 1, rows + SUB)

    def wait_edges(step, first, last):
        for flag, at_last, present in ((first, False, has_first), (last, True, has_last)):
            @pl.when(jnp.logical_and(flag, present))
            def _(at_last=at_last):
                row_copy(step, at_last).wait_recv()

    param_load.wait()

    def send_params(position, carry):
        start_sends(0, position)
        return carry

    lax.fori_loop(0, chunks, send_params, 0)
    close_edges(0, True, True)

    prev_slot = jnp.where(has_prev, 1, 0)
    next_slot = jnp.where(has_next, 2, 0)
    left_slot = jnp.where(has_left, 3, 0)
    right_slot = jnp.where(has_right, 4, 0)
    lane = lax.broadcasted_iota(jnp.int32, (SUB, cols), 1)
    level = lax.broadcasted_iota(jnp.int32, (SUB, cols), 0)
    lane_first, lane_last = lane == 0, lane == cols - 1
    level_first, level_last = level == 0, level == SUB - 1
    grid_left = lane == jnp.where(has_left, -1, 0)
    grid_right = lane == jnp.where(has_right, -1, cols - 1)

    def around(step, p, start):
        own = pl.ds(start + SUB, SUB)
        here = field[step, 0, p, own, :]
        above = field[step, 0, p, pl.ds(start, SUB), :]
        below = field[step, 0, p, pl.ds(start + 2 * SUB, SUB), :]
        up = pltpu.roll(jnp.where(level_last, above, here), 1, 0)
        down = pltpu.roll(jnp.where(level_first, below, here), SUB - 1, 0)
        left = pltpu.roll(jnp.where(lane_last, field[step, left_slot, p, own, :], here), 1, 1)
        right = pltpu.roll(
            jnp.where(lane_first, field[step, right_slot, p, own, :], here), cols - 1, 1
        )
        left = jnp.where(grid_left, here, left)
        right = jnp.where(grid_right, here, right)
        plane = (up + down) + (left + right)
        yearly = field[step, prev_slot, p, own, :] + field[step, next_slot, p, own, :]
        return here, spatial[p] * plane + temporal[p] * yearly

    def precondition(start, values):
        rows_here = pl.ds(start, SUB)
        entry = [inverse[at, rows_here, :] for at in range(len(pairs))]
        outs = []
        for p in range(count):
            total = entry[place[(0, p)]] * values[0]
            for q in range(1, count):
                total = total + entry[place[(min(p, q), max(p, q))]] * values[q]
            outs.append(total)
        return outs

    def dot(left, right):
        terms = [a * b for a, b in zip(left, right)]
        while len(terms) > 1:
            terms = [sum(terms[i : i + 2][1:], terms[i]) for i in range(0, len(terms), 2)]
        return terms[0]

    def normal(start):
        here = pl.ds(start, SUB)
        base, peak, slope, rise_mid, rise_log, fall_mid, fall_log = [
            field[0, 0, p, pl.ds(start + SUB, SUB), :] for p in range(count)
        ]
        rise_rate, fall_rate = jnp.exp(rise_log), jnp.exp(fall_log)
        rise_half, fall_half = 0.5 * rise_rate, 0.5 * fall_rate

        def date_step(date, sums):
            time = date.astype(jnp.float32) * (1.0 / dates)
            flag = qual[date, here, :].astype(jnp.float32)
            weight = jnp.maximum(1.0 - 0.5 * flag, 0.0)
            rise_gap = time - rise_mid
            fall_gap = time - fall_mid
            rise = jnp.tanh(rise_half * rise_gap)
            fall = jnp.tanh(fall_half * fall_gap)
            season = rise - fall
            height = peak - slope * time
            rise_bell = height - height * (rise * rise)
            fall_bell = height - height * (fall * fall)
            basis = [
                None,
                season,
                time * season,
                rise_bell,
                rise_gap * rise_bell,
                fall_bell,
                fall_gap * fall_bell,
            ]
            weighted = [weight] + [weight * item for item in basis[1:]]
            out = []
            for i, j in pairs:
                term = weighted[j] if i == 0 else basis[i] * weighted[j]
                out.append(sums[place[(i, j)]] + term)
            seen = obs[date, here, :]
            for i in range(count):
                out.append(sums[len(pairs) + i] + seen * weighted[i])
            return tuple(out)

        zero = jnp.zeros((SUB, cols), jnp.float32)
        sums = lax.fori_loop(
            0, dates, date_step, (zero,) * (len(pairs) + count), unroll=dates
        )
        share = land[here, :].astype(jnp.float32) * (1.0 / dates)
        rise_scale, fall_scale = 0.25 * rise_rate, 0.25 * fall_rate
        scale = [None, 0.5, -0.5, -rise_scale, rise_scale, fall_scale, -fall_scale]
        shared = [share] + [share * item for item in scale[1:]]
        block = {}
        for i, j in pairs:
            factor = shared[j] if i == 0 else shared[j] * scale[i]
            block[(i, j)] = sums[place[(i, j)]] * factor
        for p in range(count):
            total = shared[p] * sums[len(pairs) + p]
            for q, value in ((0, base), (1, peak), (2, slope)):
                total = total - block[(min(p, q), max(p, q))] * value
            resid[0, p, here, :] = total
        for p in range(count):
            block[(p, p)] = block[(p, p)] + (DAMPING + 4.0 * spatial[p] + 2.0 * temporal[p])
        for k in range(count):
            turn = 1.0 / block[(k, k)]
            edge = {i: block[(min(i, k), max(i, k))] for i in range(count) if i != k}
            lean = {i: edge[i] * turn for i in edge}
            for i, j in pairs:
                if i != k and j != k:
                    block[(i, j)] = block[(i, j)] - edge[i] * lean[j]
            for i in edge:
                block[(min(i, k), max(i, k))] = lean[i]
            block[(k, k)] = -turn
        for pair in pairs:
            inverse[place[pair], here, :] = -block[pair]

    zero = jnp.zeros((SUB, cols), jnp.float32)

    def make_stage(stage):
        def body(position, carry):
            odd_sum, even_sum = carry
            start = chunk_rows(position)
            first, last = position == 0, position == chunks - 1
            if stage == 0:
                for copy in input_loads(position):
                    copy.wait()

                def each(b, c):
                    normal(pl.multiple_of(start + b * SUB, SUB))
                    return c

                lax.fori_loop(0, BLOCKS, each, 0)
            before = stage
            wait_sides(before, position)
            wait_edges(before, first, last)
            for b in range(BLOCKS):
                at = pl.multiple_of(start + b * SUB, SUB)
                rows_here = pl.ds(at, SUB)
                held, pushed = [], []
                for p in range(count):
                    here, push = around(before, p, at)
                    if stage == 0:
                        push = (resid[0, p, rows_here, :] + push) - (
                            4.0 * spatial[p] + 2.0 * temporal[p]
                        ) * here
                    resid[stage, p, rows_here, :] = push
                    held.append(here)
                    pushed.append(push)
                if stage > 0:
                    odd_sum = odd_sum + dot(held, pushed)
                if stage < ITERS:
                    turned = precondition(at, pushed)
                    for p in range(count):
                        field[stage + 1, 0, p, pl.ds(at + SUB, SUB), :] = turned[p]
                    even_sum = even_sum + dot(turned, pushed)
            if stage < ITERS:
                start_sends(stage + 1, position)
                close_edges(stage + 1, first, last)
            return odd_sum, even_sum

        return body

    sums = []
    for stage in range(ITERS + 1):
        odd_sum, even_sum = lax.fori_loop(0, chunks, make_stage(stage), (zero, zero))
        if stage > 0:
            sums.append(odd_sum)
        if stage < ITERS:
            sums.append(even_sum)

    for at, value in enumerate(sums):
        moments[at : at + 1, :] = jnp.sum(value, axis=0, keepdims=True)

    def sum_copy(other):
        return pltpu.make_async_remote_copy(
            src_ref=moments,
            dst_ref=slots.at[other - 1],
            send_sem=sum_send.at[other - 1],
            recv_sem=sum_recv.at[other - 1],
            device_id=peer(other),
            device_id_type=MESH,
        )

    for other in range(1, total_devices):
        sum_copy(other).start()
    parts = [moments[...]]
    for other in range(1, total_devices):
        sum_copy(other).wait_recv()
        parts.append(slots[other - 1])
    while len(parts) > 1:
        parts = [sum(parts[i : i + 2][1:], parts[i]) for i in range(0, len(parts), 2)]
    total = parts[0]
    total = jnp.broadcast_to(jnp.sum(total, axis=1, keepdims=True), total.shape)
    mu = [total[at : at + 1, :] for at in range(2 * ITERS)]
    drop = [mu[at] - mu[at + 1] for at in range(2 * ITERS - 1)]

    def form(coefs, table):
        total = None
        for i, left in enumerate(coefs):
            for j in range(i, len(coefs)):
                term = left * coefs[j] * table[i + j]
                term = term if i == j else 2.0 * term
                total = term if total is None else total + term
        return total

    one = jnp.ones_like(mu[0])
    search, direction = [one], [one]
    lengths = [jnp.zeros_like(one)] * ITERS
    inner = mu[0]
    for sweep in range(ITERS):
        alpha = inner / form(direction, drop)
        for j in range(sweep + 1):
            lengths[j] = lengths[j] + alpha * direction[j]
        if sweep + 1 < ITERS:
            grown = []
            for j in range(sweep + 2):
                change = None
                if j <= sweep:
                    change = direction[j]
                if j > 0:
                    change = -direction[j - 1] if change is None else change - direction[j - 1]
                base = search[j] if j <= sweep else None
                grown.append(-alpha * change if base is None else base - alpha * change)
            search = grown
            fresh = form(search, mu)
            ratio = fresh / inner
            inner = fresh
            direction = [
                search[j] + ratio * direction[j] if j <= sweep else search[j]
                for j in range(sweep + 2)
            ]

    steps = [jnp.broadcast_to(value, (SUB, cols)) for value in lengths]
    mixes = [1.0 - steps[0]]
    mixes += [steps[j - 1] - steps[j] for j in range(1, ITERS)]
    mixes += [steps[-1]]

    def finish(b, carry):
        at = pl.multiple_of(b * SUB, SUB)
        rows_here = pl.ds(at, SUB)
        padded = pl.ds(at + SUB, SUB)
        for p in range(count):
            total = field[0, 0, p, padded, :]
            for j in range(ITERS):
                total = total + steps[j] * field[j + 1, 0, p, padded, :]
            new_params[0, p, rows_here, :] = total
            total = mixes[0] * resid[0, p, rows_here, :]
            for j in range(1, ITERS + 1):
                total = total + mixes[j] * resid[j, p, rows_here, :]
            residual[0, p, rows_here, :] = total
        return carry

    lax.fori_loop(0, rows // SUB, finish, 0)

    for step in range(ROUNDS):
        def drain(position, carry, step=step):
            for side in range(4):
                @pl.when(sides[side][0])
                def _(side=side):
                    side_copy(step, position, side).wait_send()
            return carry

        lax.fori_loop(0, chunks, drain, 0)
        for at_last, present in ((False, has_first), (True, has_last)):
            @pl.when(present)
            def _(at_last=at_last, step=step):
                row_copy(step, at_last).wait_send()
    for other in range(1, total_devices):
        sum_copy(other).wait_send()


def per_device(sizes, observed, quality, land_mask, params, spatial_weight, temporal_weight):
    n_year, n_row, n_col = sizes
    _, dates, rows, cols = observed.shape
    count = params.shape[1]
    chunks = rows // (SUB * BLOCKS)
    others = n_year * n_row * n_col - 1
    f32 = jnp.float32
    vmem = pl.BlockSpec(memory_space=pltpu.VMEM)
    hbm = pl.BlockSpec(memory_space=pltpu.HBM)
    smem = pl.BlockSpec(memory_space=pltpu.SMEM)
    dma = pltpu.SemaphoreType.DMA
    return pl.pallas_call(
        functools.partial(kernel, sizes),
        out_shape=(
            jax.ShapeDtypeStruct(params.shape, f32),
            jax.ShapeDtypeStruct(params.shape, f32),
        ),
        in_specs=[hbm, hbm, vmem, hbm, smem, smem],
        out_specs=(vmem, vmem),
        scratch_shapes=[
            pltpu.VMEM((dates, rows, cols), f32),
            pltpu.VMEM((dates, rows, cols), jnp.int32),
            pltpu.VMEM((ROUNDS, 5, count, rows + 2 * SUB, cols), f32),
            pltpu.VMEM((count * (count + 1) // 2, rows, cols), f32),
            pltpu.VMEM((ROUNDS, count, rows, cols), f32),
            pltpu.VMEM((2 * ITERS, cols), f32),
            pltpu.VMEM((max(others, 1), 2 * ITERS, cols), f32),
            dma((1 + 2 * chunks,)),
            dma((ROUNDS, 4, chunks)),
            dma((ROUNDS, 4, chunks)),
            dma((ROUNDS, 2)),
            dma((ROUNDS, 2)),
            dma((max(others, 1),)),
            dma((max(others, 1),)),
        ],
        compiler_params=pltpu.CompilerParams(
            collective_id=0, has_side_effects=True, vmem_limit_bytes=67043328
        ),
        name="gauss_newton",
    )(observed, quality, land_mask, params, spatial_weight, temporal_weight)


def solution(mesh):
    sizes = tuple(mesh.shape[axis] for axis in ("year", "row", "col"))
    grid = P("year", None, "row", "col")
    return jax.shard_map(
        functools.partial(per_device, sizes),
        mesh=mesh,
        in_specs=(grid, grid, P("row", "col"), grid, P(), P()),
        out_specs=(grid, grid),
        check_vma=False,
    )
```

```python
import functools

import jax
import jax.numpy as jnp
from jax import lax
from jax.experimental import pallas as pl
from jax.experimental.pallas import tpu as pltpu
from jax.sharding import PartitionSpec as P

ITERS = 4
ROUNDS = ITERS + 1
SUB = 8
BLOCKS = 2
DAMPING = 0.1
MESH = pl.DeviceIdType.MESH


def pairs_of(count):
    return [(i, j) for i in range(count) for j in range(i, count)]


def kernel(
    sizes,
    observed,
    quality,
    land,
    params,
    spatial,
    temporal,
    new_params,
    residual,
    obs,
    qual,
    field,
    inverse,
    resid,
    moments,
    slots,
    load_sem,
    send_sem,
    recv_sem,
    row_send,
    row_recv,
    sum_send,
    sum_recv,
):
    n_year, n_row, n_col = sizes
    dates, rows, cols = obs.shape
    count = resid.shape[1]
    step_rows = SUB * BLOCKS
    chunks = rows // step_rows
    pairs = pairs_of(count)
    place = {pair: at for at, pair in enumerate(pairs)}

    year, row, col = lax.axis_index("year"), lax.axis_index("row"), lax.axis_index("col")
    even = lax.rem(row, 2) == 0

    has_prev, has_next = year > 0, year < n_year - 1
    has_left, has_right = col > 0, col < n_col - 1
    has_up, has_down = row > 0, row < n_row - 1
    has_first = jnp.logical_or(jnp.logical_and(even, has_up), jnp.logical_and(~even, has_down))
    has_last = jnp.logical_or(jnp.logical_and(even, has_down), jnp.logical_and(~even, has_up))
    toward_first = row + jnp.where(even, -1, 1)
    toward_last = row + jnp.where(even, 1, -1)

    def chunk_rows(position):
        chunk = jnp.where(even, position, chunks - 1 - position)
        return pl.multiple_of(chunk * step_rows, step_rows)

    param_load = pltpu.make_async_copy(
        params.at[0], field.at[0, 0, :, pl.ds(SUB, rows), :], load_sem.at[0]
    )
    param_load.start()

    def input_loads(position):
        start = chunk_rows(position)
        where = (slice(None), pl.ds(start, step_rows), slice(None))
        return (
            pltpu.make_async_copy(observed.at[0].at[where], obs.at[where], load_sem.at[1 + 2 * position]),
            pltpu.make_async_copy(quality.at[0].at[where], qual.at[where], load_sem.at[2 + 2 * position]),
        )

    for position in range(chunks):
        for copy in input_loads(position):
            copy.start()

    total_devices = n_year * n_row * n_col
    near = (n_year - 1) + (n_row - 1) <= ITERS

    def peer(other):
        spot = lax.rem((year * n_row + row) * n_col + col + other, total_devices)
        return (spot // (n_row * n_col), lax.rem(spot // n_col, n_row), lax.rem(spot, n_col))

    barrier = pltpu.get_barrier_semaphore()
    if near:
        for other in range(1, n_col):
            pl.semaphore_signal(
                barrier,
                inc=1,
                device_id=(year, row, lax.rem(col + other, n_col)),
                device_id_type=MESH,
            )
        expected = n_col - 1
        for present, target in (
            (has_prev, (year - 1, row, col)),
            (has_next, (year + 1, row, col)),
            (has_up, (year, row - 1, col)),
            (has_down, (year, row + 1, col)),
        ):
            @pl.when(present)
            def _(target=target):
                pl.semaphore_signal(barrier, inc=1, device_id=target, device_id_type=MESH)

            expected = expected + present.astype(jnp.int32)
        pl.semaphore_wait(barrier, expected)
    else:
        for other in range(1, total_devices):
            pl.semaphore_signal(barrier, inc=1, device_id=peer(other), device_id_type=MESH)
        pl.semaphore_wait(barrier, total_devices - 1)

    sides = (
        (has_next, (year + 1, row, col), 1, has_prev),
        (has_prev, (year - 1, row, col), 2, has_next),
        (has_right, (year, row, col + 1), 3, has_left),
        (has_left, (year, row, col - 1), 4, has_right),
    )

    def side_copy(step, position, side):
        _, target, slot, _ = sides[side]
        where = pl.ds(chunk_rows(position) + SUB, step_rows)
        return pltpu.make_async_remote_copy(
            src_ref=field.at[step, 0, :, where, :],
            dst_ref=field.at[step, slot, :, where, :],
            send_sem=send_sem.at[step, side, position],
            recv_sem=recv_sem.at[step, side, position],
            device_id=target,
            device_id_type=MESH,
        )

    def row_copy(step, last):
        top = jnp.logical_xor(even, last)
        source = pl.multiple_of(jnp.where(top, SUB, rows), SUB)
        target = pl.multiple_of(jnp.where(top, rows + SUB, 0), SUB)
        return pltpu.make_async_remote_copy(
            src_ref=field.at[step, 0, :, pl.ds(source, SUB), :],
            dst_ref=field.at[step, 0, :, pl.ds(target, SUB), :],
            send_sem=row_send.at[step, int(last)],
            recv_sem=row_recv.at[step, int(last)],
            device_id=(year, toward_last if last else toward_first, col),
            device_id_type=MESH,
        )

    def start_sends(step, position):
        for side in range(4):
            @pl.when(sides[side][0])
            def _(side=side):
                side_copy(step, position, side).start()

    def wait_sides(step, position):
        for side in range(4):
            @pl.when(sides[side][3])
            def _(side=side):
                side_copy(step, position, side).wait_recv()

    def close_edges(step, first, last):
        for flag, at_last, present in ((first, False, has_first), (last, True, has_last)):
            top = jnp.logical_xor(even, at_last)

            @pl.when(jnp.logical_and(flag, present))
            def _(at_last=at_last):
                row_copy(step, at_last).start()

            def repeat(source, edge, target):
                for p in range(count):
                    block = field[step, 0, p, source : source + SUB, :]
                    field[step, 0, p, target : target + SUB, :] = jnp.broadcast_to(
                        block[edge : edge + 1, :], (SUB, cols)
                    )

            @pl.when(jnp.logical_and(jnp.logical_and(flag, ~present), top))
            def _():
                repeat(SUB, 0, 0)

            @pl.when(jnp.logical_and(jnp.logical_and(flag, ~present), ~top))
            def _():
                repeat(rows, SUB - 1, rows + SUB)

    def wait_edges(step, first, last):
        for flag, at_last, present in ((first, False, has_first), (last, True, has_last)):
            @pl.when(jnp.logical_and(flag, present))
            def _(at_last=at_last):
                row_copy(step, at_last).wait_recv()

    param_load.wait()

    def send_params(position, carry):
        start_sends(0, position)
        return carry

    lax.fori_loop(0, chunks, send_params, 0)
    close_edges(0, True, True)

    prev_slot = jnp.where(has_prev, 1, 0)
    next_slot = jnp.where(has_next, 2, 0)
    left_slot = jnp.where(has_left, 3, 0)
    right_slot = jnp.where(has_right, 4, 0)
    lane = lax.broadcasted_iota(jnp.int32, (SUB, cols), 1)
    level = lax.broadcasted_iota(jnp.int32, (SUB, cols), 0)
    lane_first, lane_last = lane == 0, lane == cols - 1
    level_first, level_last = level == 0, level == SUB - 1
    grid_left = lane == jnp.where(has_left, -1, 0)
    grid_right = lane == jnp.where(has_right, -1, cols - 1)

    def around(step, p, start):
        own = pl.ds(start + SUB, SUB)
        here = field[step, 0, p, own, :]
        above = field[step, 0, p, pl.ds(start, SUB), :]
        below = field[step, 0, p, pl.ds(start + 2 * SUB, SUB), :]
        up = pltpu.roll(jnp.where(level_last, above, here), 1, 0)
        down = pltpu.roll(jnp.where(level_first, below, here), SUB - 1, 0)
        left = pltpu.roll(jnp.where(lane_last, field[step, left_slot, p, own, :], here), 1, 1)
        right = pltpu.roll(
            jnp.where(lane_first, field[step, right_slot, p, own, :], here), cols - 1, 1
        )
        left = jnp.where(grid_left, here, left)
        right = jnp.where(grid_right, here, right)
        plane = (up + down) + (left + right)
        yearly = field[step, prev_slot, p, own, :] + field[step, next_slot, p, own, :]
        return here, spatial[p] * plane + temporal[p] * yearly

    def precondition(start, values):
        rows_here = pl.ds(start, SUB)
        entry = [inverse[at, rows_here, :] for at in range(len(pairs))]
        outs = []
        for p in range(count):
            total = entry[place[(0, p)]] * values[0]
            for q in range(1, count):
                total = total + entry[place[(min(p, q), max(p, q))]] * values[q]
            outs.append(total)
        return outs

    def dot(left, right):
        terms = [a * b for a, b in zip(left, right)]
        while len(terms) > 1:
            terms = [sum(terms[i : i + 2][1:], terms[i]) for i in range(0, len(terms), 2)]
        return terms[0]

    def normal(start):
        here = pl.ds(start, SUB)
        base, peak, slope, rise_mid, rise_log, fall_mid, fall_log = [
            field[0, 0, p, pl.ds(start + SUB, SUB), :] for p in range(count)
        ]
        rise_rate, fall_rate = jnp.exp(rise_log), jnp.exp(fall_log)
        rise_half, fall_half = 0.5 * rise_rate, 0.5 * fall_rate

        def date_step(date, sums):
            time = date.astype(jnp.float32) * (1.0 / dates)
            flag = qual[date, here, :].astype(jnp.float32)
            weight = jnp.maximum(1.0 - 0.5 * flag, 0.0)
            rise_gap = time - rise_mid
            fall_gap = time - fall_mid
            rise = jnp.tanh(rise_half * rise_gap)
            fall = jnp.tanh(fall_half * fall_gap)
            season = rise - fall
            height = peak - slope * time
            rise_bell = height - height * (rise * rise)
            fall_bell = height - height * (fall * fall)
            basis = [
                None,
                season,
                time * season,
                rise_bell,
                rise_gap * rise_bell,
                fall_bell,
                fall_gap * fall_bell,
            ]
            weighted = [weight] + [weight * item for item in basis[1:]]
            out = []
            for i, j in pairs:
                term = weighted[j] if i == 0 else basis[i] * weighted[j]
                out.append(sums[place[(i, j)]] + term)
            seen = obs[date, here, :]
            for i in range(count):
                out.append(sums[len(pairs) + i] + seen * weighted[i])
            return tuple(out)

        zero = jnp.zeros((SUB, cols), jnp.float32)
        sums = lax.fori_loop(
            0, dates, date_step, (zero,) * (len(pairs) + count), unroll=dates
        )
        share = land[here, :].astype(jnp.float32) * (1.0 / dates)
        rise_scale, fall_scale = 0.25 * rise_rate, 0.25 * fall_rate
        scale = [None, 0.5, -0.5, -rise_scale, rise_scale, fall_scale, -fall_scale]
        shared = [share] + [share * item for item in scale[1:]]
        block = {}
        for i, j in pairs:
            factor = shared[j] if i == 0 else shared[j] * scale[i]
            block[(i, j)] = sums[place[(i, j)]] * factor
        for p in range(count):
            total = shared[p] * sums[len(pairs) + p]
            for q, value in ((0, base), (1, peak), (2, slope)):
                total = total - block[(min(p, q), max(p, q))] * value
            resid[0, p, here, :] = total
        for p in range(count):
            block[(p, p)] = block[(p, p)] + (DAMPING + 4.0 * spatial[p] + 2.0 * temporal[p])
        for k in range(count):
            turn = 1.0 / block[(k, k)]
            edge = {i: block[(min(i, k), max(i, k))] for i in range(count) if i != k}
            lean = {i: edge[i] * turn for i in edge}
            for i, j in pairs:
                if i != k and j != k:
                    block[(i, j)] = block[(i, j)] - edge[i] * lean[j]
            for i in edge:
                block[(min(i, k), max(i, k))] = lean[i]
            block[(k, k)] = -turn
        for pair in pairs:
            inverse[place[pair], here, :] = -block[pair]

    zero = jnp.zeros((SUB, cols), jnp.float32)

    def make_stage(stage):
        def body(position, carry):
            odd_sum, even_sum = carry
            start = chunk_rows(position)
            first, last = position == 0, position == chunks - 1
            if stage == 0:
                for copy in input_loads(position):
                    copy.wait()

                def each(b, c):
                    normal(pl.multiple_of(start + b * SUB, SUB))
                    return c

                lax.fori_loop(0, BLOCKS, each, 0)
            before = stage
            wait_sides(before, position)
            wait_edges(before, first, last)
            for b in range(BLOCKS):
                at = pl.multiple_of(start + b * SUB, SUB)
                rows_here = pl.ds(at, SUB)
                held, pushed = [], []
                for p in range(count):
                    here, push = around(before, p, at)
                    if stage == 0:
                        push = (resid[0, p, rows_here, :] + push) - (
                            4.0 * spatial[p] + 2.0 * temporal[p]
                        ) * here
                    resid[stage, p, rows_here, :] = push
                    held.append(here)
                    pushed.append(push)
                if stage > 0:
                    odd_sum = odd_sum + dot(held, pushed)
                if stage < ITERS:
                    turned = precondition(at, pushed)
                    for p in range(count):
                        field[stage + 1, 0, p, pl.ds(at + SUB, SUB), :] = turned[p]
                    even_sum = even_sum + dot(turned, pushed)
            if stage < ITERS:
                start_sends(stage + 1, position)
                close_edges(stage + 1, first, last)
            return odd_sum, even_sum

        return body

    sums = []
    for stage in range(ITERS + 1):
        odd_sum, even_sum = lax.fori_loop(0, chunks, make_stage(stage), (zero, zero))
        if stage > 0:
            sums.append(odd_sum)
        if stage < ITERS:
            sums.append(even_sum)

    for at, value in enumerate(sums):
        moments[at : at + 1, :] = jnp.sum(value, axis=0, keepdims=True)

    def sum_copy(other):
        return pltpu.make_async_remote_copy(
            src_ref=moments,
            dst_ref=slots.at[other - 1],
            send_sem=sum_send.at[other - 1],
            recv_sem=sum_recv.at[other - 1],
            device_id=peer(other),
            device_id_type=MESH,
        )

    for other in range(1, total_devices):
        sum_copy(other).start()
    for step in range(ROUNDS):
        def drain(position, carry, step=step):
            for side in range(4):
                @pl.when(sides[side][0])
                def _(side=side):
                    side_copy(step, position, side).wait_send()
            return carry

        lax.fori_loop(0, chunks, drain, 0)
        for at_last, present in ((False, has_first), (True, has_last)):
            @pl.when(present)
            def _(at_last=at_last, step=step):
                row_copy(step, at_last).wait_send()
    parts = [moments[...]]
    for other in range(1, total_devices):
        sum_copy(other).wait_recv()
        parts.append(slots[other - 1])
    while len(parts) > 1:
        parts = [sum(parts[i : i + 2][1:], parts[i]) for i in range(0, len(parts), 2)]
    total = parts[0]
    total = jnp.broadcast_to(jnp.sum(total, axis=1, keepdims=True), total.shape)
    mu = [total[at : at + 1, :] for at in range(2 * ITERS)]
    drop = [mu[at] - mu[at + 1] for at in range(2 * ITERS - 1)]

    def form(coefs, table):
        total = None
        for i, left in enumerate(coefs):
            for j in range(i, len(coefs)):
                term = left * coefs[j] * table[i + j]
                term = term if i == j else 2.0 * term
                total = term if total is None else total + term
        return total

    one = jnp.ones_like(mu[0])
    search, direction = [one], [one]
    lengths = [jnp.zeros_like(one)] * ITERS
    inner = mu[0]
    for sweep in range(ITERS):
        alpha = inner / form(direction, drop)
        for j in range(sweep + 1):
            lengths[j] = lengths[j] + alpha * direction[j]
        if sweep + 1 < ITERS:
            grown = []
            for j in range(sweep + 2):
                change = None
                if j <= sweep:
                    change = direction[j]
                if j > 0:
                    change = -direction[j - 1] if change is None else change - direction[j - 1]
                base = search[j] if j <= sweep else None
                grown.append(-alpha * change if base is None else base - alpha * change)
            search = grown
            fresh = form(search, mu)
            ratio = fresh / inner
            inner = fresh
            direction = [
                search[j] + ratio * direction[j] if j <= sweep else search[j]
                for j in range(sweep + 2)
            ]

    steps = [jnp.broadcast_to(value, (SUB, cols)) for value in lengths]
    mixes = [1.0 - steps[0]]
    mixes += [steps[j - 1] - steps[j] for j in range(1, ITERS)]
    mixes += [steps[-1]]

    def finish(b, carry):
        at = pl.multiple_of(b * SUB, SUB)
        rows_here = pl.ds(at, SUB)
        padded = pl.ds(at + SUB, SUB)
        for p in range(count):
            total = field[0, 0, p, padded, :]
            for j in range(ITERS):
                total = total + steps[j] * field[j + 1, 0, p, padded, :]
            new_params[0, p, rows_here, :] = total
            total = mixes[0] * resid[0, p, rows_here, :]
            for j in range(1, ITERS + 1):
                total = total + mixes[j] * resid[j, p, rows_here, :]
            residual[0, p, rows_here, :] = total
        return carry

    lax.fori_loop(0, rows // SUB, finish, 0)

    for other in range(1, total_devices):
        sum_copy(other).wait_send()


def per_device(sizes, observed, quality, land_mask, params, spatial_weight, temporal_weight):
    n_year, n_row, n_col = sizes
    _, dates, rows, cols = observed.shape
    count = params.shape[1]
    chunks = rows // (SUB * BLOCKS)
    others = n_year * n_row * n_col - 1
    f32 = jnp.float32
    vmem = pl.BlockSpec(memory_space=pltpu.VMEM)
    hbm = pl.BlockSpec(memory_space=pltpu.HBM)
    smem = pl.BlockSpec(memory_space=pltpu.SMEM)
    dma = pltpu.SemaphoreType.DMA
    return pl.pallas_call(
        functools.partial(kernel, sizes),
        out_shape=(
            jax.ShapeDtypeStruct(params.shape, f32),
            jax.ShapeDtypeStruct(params.shape, f32),
        ),
        in_specs=[hbm, hbm, vmem, hbm, smem, smem],
        out_specs=(vmem, vmem),
        scratch_shapes=[
            pltpu.VMEM((dates, rows, cols), f32),
            pltpu.VMEM((dates, rows, cols), jnp.int32),
            pltpu.VMEM((ROUNDS, 5, count, rows + 2 * SUB, cols), f32),
            pltpu.VMEM((count * (count + 1) // 2, rows, cols), f32),
            pltpu.VMEM((ROUNDS, count, rows, cols), f32),
            pltpu.VMEM((2 * ITERS, cols), f32),
            pltpu.VMEM((max(others, 1), 2 * ITERS, cols), f32),
            dma((1 + 2 * chunks,)),
            dma((ROUNDS, 4, chunks)),
            dma((ROUNDS, 4, chunks)),
            dma((ROUNDS, 2)),
            dma((ROUNDS, 2)),
            dma((max(others, 1),)),
            dma((max(others, 1),)),
        ],
        compiler_params=pltpu.CompilerParams(
            collective_id=0, has_side_effects=True, vmem_limit_bytes=67043328
        ),
        name="gauss_newton",
    )(observed, quality, land_mask, params, spatial_weight, temporal_weight)


def solution(mesh):
    sizes = tuple(mesh.shape[axis] for axis in ("year", "row", "col"))
    grid = P("year", None, "row", "col")
    return jax.shard_map(
        functools.partial(per_device, sizes),
        mesh=mesh,
        in_specs=(grid, grid, P("row", "col"), grid, P(), P()),
        out_specs=(grid, grid),
        check_vma=False,
    )
```
